256 devices in a mesh: ctx: 64 (over x, z, core), tp: 4 (over y).
Axes of the slice: x: 4, y: 4, z: 8, core: 2. Of those that a mesh axis runs over, the one named last changes fastest.
Arguments:
- tokens_in: bfloat16 [32768, 2048], P('ctx'), may hold values from -6 to 6
- w_query: bfloat16 [2048, 2048], P(None, 'tp'), may hold values from -0.125 to 0.125
- w_key: bfloat16 [2048, 2048], P(None, 'tp'), may hold values from -0.125 to 0.125
- w_value: bfloat16 [2048, 2048], P(None, 'tp'), may hold values from -0.125 to 0.125
- grad_out: bfloat16 [32768, 2048], P('ctx', 'tp'), may hold values from -4 to 4
- trajectory_ends: int32 [32768], P('ctx'), may hold values from 0 to 1, as said below
Outputs:
- grad_tokens: bfloat16 [32768, 2048], P(('ctx', 'tp'))
The draws below stay inside these ranges and needn't reach their ends.
Inputs may be any that keep to these rules, and one draw needn't show every extreme that they name: `trajectory_ends`: 1 marks a token that ends a trajectory, 0 any other token; trajectories may span many blocks.
All inputs are finite; a program needn't handle non-finite values.
Results may differ from the reference program's by a relative error of at most 0.0061.
Values sent between devices are 32-bit elements; how exact they have to be, the bound alone decides.
No kernel may reach another device: no remote copies, remote signals or barrier semaphores. Data moves between devices by JAX's collectives and lax.ppermute only.
A program may use at most 128 MiB of HBM per device.

```python
import jax
import jax.numpy as jnp
from jax import lax

D = 2048
HEADS = 16
HD = 128
TOK_DEV = 512
TOKENS = 32768


def draw_trajectory_ends(key, part):
    blocks = TOKENS // TOK_DEV
    key_count, key_place, key_span, key_start = jax.random.split(jax.random.fold_in(key, 17), 4)
    span_blocks = blocks // 2 + jax.random.randint(key_span, (), 0, blocks // 4 + 1)
    first_block = jax.random.randint(key_start, (), 0, blocks - span_blocks + 1)
    block_ids = jnp.arange(blocks)
    inside = (block_ids >= first_block) & (block_ids < first_block + span_blocks)
    counts = jnp.maximum(jax.random.randint(key_count, (blocks, 1), 0, 6) - 2, 0)
    counts = jnp.where(inside[:, None], 0, counts)
    places = jax.random.randint(key_place, (blocks, 3), 0, TOK_DEV)
    active = jnp.arange(3)[None, :] < counts
    column = jnp.arange(TOK_DEV)
    struck = jnp.any((places[:, :, None] == column[None, None, :]) & active[:, :, None], axis=1)
    return struck.astype(jnp.int32).reshape(TOKENS)


def levels(rng, dims, cuts, least, largest):
    factor_of = 1.0
    for dim, shards_of in cuts:
        steps = jax.random.uniform(jax.random.fold_in(jax.random.fold_in(rng, 6), dim), (shards_of,), jnp.float32, least / len(cuts), largest / len(cuts))
        factor_of = factor_of * jnp.repeat(jnp.exp(steps), dims[dim] // shards_of).reshape((-1,) + (1,) * (len(dims) - 1 - dim))
    return factor_of


def bell_draw(stream_key, shape, scale, limit, pieces=(), kind=jnp.bfloat16):
    result = scale * jax.random.normal(stream_key, shape, jnp.float32)
    if pieces:
        result = result * levels(stream_key, shape, pieces, -0.22, 0.18)
    return jnp.clip(result, -limit, limit).astype(kind)


def setup_inputs(seed: int = 0) -> dict:
    key_of = jax.random.split(jax.random.key(seed), 7)
    return {
        "tokens_in": bell_draw(key_of[0], (TOKENS, D), 1.0, 6.0, ((0, 64),)),
        "w_query": bell_draw(key_of[1], (D, HEADS * HD), D ** -0.5, 0.125, ((1, 4),)),
        "w_key": bell_draw(key_of[2], (D, HEADS * HD), D ** -0.5, 0.125, ((1, 4),)),
        "w_value": bell_draw(key_of[3], (D, HEADS * HD), D ** -0.5, 0.125, ((1, 4),)),
        "grad_out": bell_draw(key_of[4], (TOKENS, HEADS * HD), 0.3, 4.0, ((0, 64), (1, 4))),
        "trajectory_ends": draw_trajectory_ends(jax.random.fold_in(key_of[6], 71), 0),
    }


def joined(earlier, later):
    return (later[0] + (1.0 - later[1][0]) * earlier[0], jnp.maximum(earlier[1], later[1]))


def block_masks(end_flags):
    count = end_flags.shape[0]
    before = (jnp.cumsum(end_flags) - end_flags).astype(jnp.int32)
    end_total = jnp.sum(end_flags).astype(jnp.int32)
    opened = (before == 0)
    closed = (end_total - before == 0)
    positions = jnp.arange(count, dtype=jnp.int32)
    pair_mask = (positions[None, :] <= positions[:, None]) & (before[:, None] == before[None, :])
    reset_any = (end_total > 0).astype(jnp.float32).reshape(1)
    return opened, closed, pair_mask, reset_any


def block_summary(queries, key_rows, value_rows, grad_rows, end_flags):
    opened, closed, pair_mask, reset_any = block_masks(end_flags)
    later_vals = value_rows.astype(jnp.float32) * closed[:, None, None].astype(jnp.float32)
    first_grads = grad_rows.astype(jnp.float32) * opened[:, None, None].astype(jnp.float32)
    carry_out = jnp.einsum('shv,shk->hvk', later_vals, key_rows.astype(jnp.float32))
    grads_out = jnp.einsum('thv,thk->hvk', first_grads, queries.astype(jnp.float32))
    return carry_out, grads_out, reset_any


def block_grads(queries, key_rows, value_rows, grad_rows, end_flags, state_in, grads_in):
    opened, closed, pair_mask, reset_any = block_masks(end_flags)
    qf = queries.astype(jnp.float32)
    kf = key_rows.astype(jnp.float32)
    vf = value_rows.astype(jnp.float32)
    gf = grad_rows.astype(jnp.float32)
    scores = jnp.einsum('thv,shv->hts', gf, vf)
    scores = jnp.where(pair_mask[None], scores, 0.0).astype(jnp.bfloat16).astype(jnp.float32)
    attn = jnp.einsum('thk,shk->hts', qf, kf)
    attn = jnp.where(pair_mask[None], attn, 0.0).astype(jnp.bfloat16).astype(jnp.float32)
    state_bf = state_in.astype(jnp.bfloat16).astype(jnp.float32)
    grads_bf = grads_in.astype(jnp.bfloat16).astype(jnp.float32)
    open_f = opened.astype(jnp.float32)[:, None, None]
    close_f = closed.astype(jnp.float32)[:, None, None]
    score_scale = 1.0 / queries.shape[-1]
    dq = jnp.einsum('hts,shk->thk', scores, kf) + open_f * jnp.einsum('thv,hvk->thk', gf, state_bf)
    dk = jnp.einsum('hts,thk->shk', scores, qf) + close_f * jnp.einsum('shv,hvk->shk', vf, grads_bf)
    dv = jnp.einsum('hts,thv->shv', attn, gf) + close_f * jnp.einsum('shk,hvk->shv', kf, grads_bf)
    return ((score_scale * dq).astype(jnp.bfloat16), (score_scale * dk).astype(jnp.bfloat16),
            (score_scale * dv).astype(jnp.bfloat16))


def reference(tokens_in, w_query, w_key, w_value, grad_out, trajectory_ends):
    blocks = TOKENS // TOK_DEV
    shape = (blocks, TOK_DEV, HEADS, HD)
    queries = jnp.dot(tokens_in, w_query, preferred_element_type=jnp.float32).astype(jnp.bfloat16).reshape(shape)
    key_rows = jnp.dot(tokens_in, w_key, preferred_element_type=jnp.float32).astype(jnp.bfloat16).reshape(shape)
    value_rows = jnp.dot(tokens_in, w_value, preferred_element_type=jnp.float32).astype(jnp.bfloat16).reshape(shape)
    grad_rows = grad_out.reshape(shape)
    end_flags = trajectory_ends.reshape(blocks, TOK_DEV)
    carry_out, grads_out, reset_any = jax.vmap(block_summary)(queries, key_rows, value_rows, grad_rows, end_flags)

    def advance(carry, item):
        return joined(carry, item), carry[0]

    empty = (jnp.zeros((HEADS, HD, HD), jnp.float32), jnp.zeros((1,), jnp.float32))
    _, state_in = lax.scan(advance, empty, (carry_out, reset_any))
    _, grads_in = lax.scan(advance, empty, (grads_out, reset_any), reverse=True)
    dq, dk, dv = jax.vmap(block_grads)(queries, key_rows, value_rows, grad_rows, end_flags, state_in, grads_in)
    flat = (TOKENS, HEADS * HD)
    total = jnp.dot(dq.reshape(flat), w_query.T, preferred_element_type=jnp.float32)
    total = total + jnp.dot(dk.reshape(flat), w_key.T, preferred_element_type=jnp.float32)
    total = total + jnp.dot(dv.reshape(flat), w_value.T, preferred_element_type=jnp.float32)
    return total.astype(jnp.bfloat16)
```

```python
import jax
import jax.numpy as jnp
from jax import lax
from jax.sharding import PartitionSpec as P

HD = 128


def ring(count, step):
    return [(i, (i + step) % count) for i in range(count)]


def carried(a_own, b_own, reset):
    devices = lax.axis_size("ctx")
    chips = devices // 2
    core = lax.axis_index("ctx") % 2
    first = core == 0
    pairs = [(i, i ^ 1) for i in range(devices)]
    groups = [[2 * j + c for j in range(chips)] for c in range(2)]
    heads = a_own.shape[0]
    half = heads // 2
    size = half * HD * HD
    lane = (chips, size // chips)

    def part(a, which):
        return lax.dynamic_slice_in_dim(a, which * half, half, 0)

    flags = jnp.broadcast_to(reset, (8, HD))
    flat = (-1, HD)
    away = jnp.concatenate([a_own.reshape(flat), b_own.reshape(flat), flags], 0)
    other = lax.ppermute(away, "ctx", pairs)
    rows = heads * HD
    a_other = other[:rows].reshape(a_own.shape)
    b_other = other[rows : 2 * rows].reshape(b_own.shape)
    r_other = other[2 * rows, 0]
    a_mine, b_mine = part(a_own, core), part(b_own, core)
    a_theirs, b_theirs = part(a_other, core), part(b_other, core)
    left = 1.0 - reset
    left_other = 1.0 - r_other
    a_chip = jnp.where(first, a_theirs + left_other * a_mine, a_mine + left * a_theirs)
    b_chip = jnp.where(first, b_mine + left * b_theirs, b_theirs + left_other * b_mine)
    r_chip = jnp.broadcast_to(jnp.maximum(reset, r_other), (chips, HD))
    out = jnp.concatenate([a_chip.reshape(lane), b_chip.reshape(lane), r_chip], 1)
    got = lax.all_to_all(out, "ctx", 0, 0, axis_index_groups=groups, tiled=True)
    width = lane[1]
    r = got[:, 2 * width]
    place = jnp.arange(chips)
    upto = jnp.sum(jnp.where(place[None, :] <= place[:, None], r[None, :], 0.0), 1)
    below = upto - r
    lower = ((place[None, :] < place[:, None]) & (below[:, None] == upto[None, :])).astype(jnp.float32)
    upper = ((place[None, :] > place[:, None]) & (below[None, :] == upto[:, None])).astype(jnp.float32)
    high = lax.Precision.HIGHEST
    a_in = jnp.dot(lower, got[:, :width], precision=high)
    b_in = jnp.dot(upper, got[:, width : 2 * width], precision=high)
    back = lax.all_to_all(
        jnp.concatenate([a_in, b_in], 1), "ctx", 0, 0, axis_index_groups=groups, tiled=True
    )
    mine = jnp.concatenate([back[:, :width].reshape(flat), back[:, width:].reshape(flat)], 0)
    theirs = lax.ppermute(mine, "ctx", pairs)
    low = jnp.where(first, mine, theirs)
    top = jnp.where(first, theirs, mine)
    rows = half * HD
    a_pre = jnp.concatenate([low[:rows], top[:rows]], 0).reshape(a_own.shape)
    b_pre = jnp.concatenate([low[rows:], top[rows:]], 0).reshape(b_own.shape)
    is_one = core.astype(jnp.float32)
    is_zero = 1.0 - is_one
    a_in = is_one * a_other + (1.0 - is_one * r_other) * a_pre
    b_in = is_zero * b_other + (1.0 - is_zero * r_other) * b_pre
    return a_in, b_in


def body(tokens_in, w_query, w_key, w_value, grad_out, trajectory_ends):
    row_count = tokens_in.shape[0]
    head_count = w_query.shape[1] // HD
    shape = (row_count, head_count, HD)
    f32 = jnp.float32

    def project(weight):
        return jnp.dot(tokens_in, weight, preferred_element_type=f32).astype(jnp.bfloat16).reshape(shape)

    before_f = trajectory_ends.astype(f32)
    positions = jnp.arange(row_count, dtype=jnp.int32)
    below = positions[None, :] < positions[:, None]
    before = jnp.sum(jnp.where(below, before_f[None, :], 0.0), axis=1)
    end_total = jnp.sum(before_f)
    opened = before == 0
    closed = end_total - before == 0
    pair_mask = (positions[None, :] <= positions[:, None]) & (before[:, None] == before[None, :])
    reset = (end_total > 0).astype(f32)
    open_bf = opened.astype(jnp.bfloat16)[:, None, None]
    close_bf = closed.astype(jnp.bfloat16)[:, None, None]
    grad_rows = grad_out.reshape(shape)
    key_rows = project(w_key)
    value_rows = project(w_value)
    queries = project(w_query)
    carry_out = jnp.einsum("shv,shk->hvk", value_rows * close_bf, key_rows, preferred_element_type=f32)
    grads_out = jnp.einsum("thv,thk->hvk", grad_rows * open_bf, queries, preferred_element_type=f32)
    state_in, grads_in = carried(carry_out, grads_out, reset)

    scores = jnp.einsum("thv,shv->hts", grad_rows, value_rows, preferred_element_type=f32)
    scores = jnp.where(pair_mask[None], scores, 0.0).astype(jnp.bfloat16)
    attn = jnp.einsum("thk,shk->hts", queries, key_rows, preferred_element_type=f32)
    attn = jnp.where(pair_mask[None], attn, 0.0).astype(jnp.bfloat16)
    state_bf = state_in.astype(jnp.bfloat16)
    grads_bf = grads_in.astype(jnp.bfloat16)
    open_f = opened.astype(f32)[:, None, None]
    close_f = closed.astype(f32)[:, None, None]
    scale = 1.0 / HD
    grad_query = jnp.einsum("hts,shk->thk", scores, key_rows, preferred_element_type=f32)
    grad_query = grad_query + open_f * jnp.einsum("thv,hvk->thk", grad_rows, state_bf, preferred_element_type=f32)
    grad_key = jnp.einsum("hts,thk->shk", scores, queries, preferred_element_type=f32)
    grad_key = grad_key + close_f * jnp.einsum("shv,hvk->shk", value_rows, grads_bf, preferred_element_type=f32)
    grad_value = jnp.einsum("hts,thv->shv", attn, grad_rows, preferred_element_type=f32)
    grad_value = grad_value + close_f * jnp.einsum("shk,hvk->shv", key_rows, grads_bf, preferred_element_type=f32)
    flat = (row_count, head_count * HD)
    grad_query = (scale * grad_query).astype(jnp.bfloat16).reshape(flat)
    grad_key = (scale * grad_key).astype(jnp.bfloat16).reshape(flat)
    grad_value = (scale * grad_value).astype(jnp.bfloat16).reshape(flat)

    shards = lax.axis_size("tp")
    me = lax.axis_index("tp")
    rows = row_count // shards
    dims = (((1,), (1,)), ((), ()))

    def chunk(offset):
        start = (me + offset) % shards * rows

        def piece(a, weight):
            return lax.dot_general(
                lax.dynamic_slice_in_dim(a, start, rows, 0), weight, dims, preferred_element_type=f32
            )

        return piece(grad_query, w_query) + piece(grad_key, w_key) + piece(grad_value, w_value)

    split = rows // 2
    up, down = ring(shards, 1), ring(shards, -1)
    far = chunk(2)
    far_up = lax.ppermute(far[:split], "tp", up)
    far_down = lax.ppermute(far[split:], "tp", down)
    above, under = chunk(1), chunk(3)
    near_up = lax.ppermute(above[split:], "tp", up)
    near_down = lax.ppermute(under[:split], "tp", down)
    own = chunk(0)
    last_up = lax.ppermute(above[:split] + far_up, "tp", up)
    last_down = lax.ppermute(under[split:] + far_down, "tp", down)
    low = own[:split] + near_down + last_up
    top = own[split:] + near_up + last_down
    return jnp.concatenate([low, top], 0).astype(jnp.bfloat16)


def solution(mesh):
    return jax.shard_map(
        body,
        mesh=mesh,
        in_specs=(
            P("ctx", None),
            P(None, "tp"),
            P(None, "tp"),
            P(None, "tp"),
            P("ctx", "tp"),
            P("ctx"),
        ),
        out_specs=P(("ctx", "tp"), None),
        check_vma=False,
    )
```

```python
import jax
import jax.numpy as jnp
from jax import lax
from jax.experimental import pallas as pl
from jax.experimental.pallas import tpu as pltpu
from jax.sharding import PartitionSpec as P

HD = 128
F32 = jnp.float32
BF16 = jnp.bfloat16
MIB = 1 << 20
NT = (((1,), (1,)), ((), ()))
TN = (((0,), (0,)), ((), ()))
VM = pltpu.VMEM


def whole():
    return pl.BlockSpec(memory_space=pltpu.VMEM)


def params(mib, **more):
    return pltpu.CompilerParams(vmem_limit_bytes=mib * MIB, **more)


def cost(flops, moved):
    return pl.CostEstimate(flops=int(flops), bytes_accessed=int(moved), transcendentals=0)


def ring(count, step):
    return [(i, (i + step) % count) for i in range(count)]


def nt(a, b):
    return lax.dot_general(a, b, NT, preferred_element_type=F32)


def tn(a, b):
    return lax.dot_general(a, b, TN, preferred_element_type=F32)


def nn(a, b):
    return jnp.dot(a, b, preferred_element_type=F32)


def ends_before(ends):
    n = ends.shape[1]
    row = lax.broadcasted_iota(jnp.int32, (n, n), 0)
    col = lax.broadcasted_iota(jnp.int32, (n, n), 1)
    return jnp.sum(jnp.where(col < row, ends, 0.0), axis=1, keepdims=True)


def project_kernel(x, wq, wk, wv, g, e, q, k, v, msg, xs, ws, gs, acc, stage, in_sem, g_sem, out_sem):
    deep = xs.shape[2]
    steps = xs.shape[0]
    cols = acc.shape[1] // 3
    heads = cols // HD

    def loads(step):
        at = pl.ds(step * deep, deep)
        pairs = [(x.at[:, at], xs.at[step])]
        pairs += [(w.at[at, :], ws.at[step, :, pl.ds(i * cols, cols)]) for i, w in enumerate((wq, wk, wv))]
        return [pltpu.make_async_copy(a, b, in_sem.at[step, i]) for i, (a, b) in enumerate(pairs)]

    for step in range(steps):
        for copy in loads(step):
            copy.start()
    grad = pltpu.make_async_copy(g, gs, g_sem)
    grad.start()
    ends = e[...].astype(F32)
    before = ends_before(ends)
    total = jnp.sum(ends, axis=1, keepdims=True)
    opened = (before == 0.0).astype(F32)
    closed = (total == before).astype(F32)
    msg[2 * heads * HD :, :] = jnp.broadcast_to((total > 0.0).astype(F32), (8, HD))
    for step in range(steps):
        for copy in loads(step):
            copy.wait()
        part = nn(xs[step], ws[step])
        if step == 0:
            acc[...] = part
        elif step < steps - 1:
            acc[...] += part
    last = acc[...] + part
    grad.wait()
    saved = []
    for i in (1, 2, 0):
        stage[i] = last[:, i * cols : (i + 1) * cols].astype(BF16)
        copy = pltpu.make_async_copy(stage.at[i], (q, k, v)[i], out_sem.at[i])
        copy.start()
        saved.append(copy)
    for h in range(heads):
        at = slice(h * HD, (h + 1) * HD)
        vmb = (stage[2, :, at].astype(F32) * closed).astype(BF16)
        msg[at, :] = tn(vmb, stage[1, :, at])
        gmb = (gs[:, at].astype(F32) * opened).astype(BF16)
        msg[(heads + h) * HD : (heads + h + 1) * HD, :] = tn(gmb, stage[0, :, at])
    for copy in saved:
        copy.wait()


def project(x, wq, wk, wv, g, ends):
    rows, width = x.shape
    cols = wq.shape[1]
    steps = 4
    deep = width // steps
    hbm = pl.BlockSpec(memory_space=pltpu.HBM)
    out = jax.ShapeDtypeStruct((rows, cols), BF16)
    dma = pltpu.SemaphoreType.DMA
    return pl.pallas_call(
        project_kernel,
        in_specs=[hbm] * 5 + [whole()],
        out_specs=[hbm] * 3 + [whole()],
        out_shape=[out] * 3 + [jax.ShapeDtypeStruct((2 * cols + 8, HD), F32)],
        scratch_shapes=[
            VM((steps, rows, deep), BF16),
            VM((steps, deep, 3 * cols), BF16),
            VM((rows, cols), BF16),
            VM((rows, 3 * cols), F32),
            VM((3, rows, cols), BF16),
            dma((steps, 4)),
            dma,
            dma((3,)),
        ],
        compiler_params=params(62),
        cost_estimate=cost(6 * rows * width * cols, 2 * (rows * width + 3 * width * cols)),
        name="project",
    )(x, wq, wk, wv, g, ends)


def fold_kernel(mine, other, out):
    core = lax.rem(lax.axis_index("ctx"), 2)
    rows = (mine.shape[0] - 8) // 2
    half = rows // 2
    chips = half // 8
    unit = out.shape[0] // chips
    own_r = mine[2 * rows : 2 * rows + 1, :]
    far_r = other[2 * rows : 2 * rows + 1, :]
    is_one = core.astype(F32)
    is_zero = 1.0 - is_one
    own_a = 1.0 - is_zero * far_r
    far_a = 1.0 - is_one * own_r
    own_b = 1.0 - is_one * far_r
    far_b = 1.0 - is_zero * own_r
    flag = jnp.maximum(own_r, far_r)
    base = pl.multiple_of(core * half, 8)
    for j in range(chips):
        a = pl.ds(base + 8 * j, 8)
        b = pl.ds(base + rows + 8 * j, 8)
        out[unit * j : unit * j + 8, :] = own_a * mine[a, :] + far_a * other[a, :]
        out[unit * j + 8 : unit * j + 16, :] = own_b * mine[b, :] + far_b * other[b, :]
        out[unit * j + 16 : unit * j + 24, :] = jnp.broadcast_to(flag, (8, HD))


def fold(mine, other):
    half = (mine.shape[0] - 8) // 4
    return pl.pallas_call(
        fold_kernel,
        in_specs=[whole(), whole()],
        out_specs=whole(),
        out_shape=jax.ShapeDtypeStruct((half // 8 * 24, HD), F32),
        compiler_params=params(8),
        cost_estimate=cost(half * HD * 8, mine.size * 8),
        name="fold",
    )(mine, other)


def scan_kernel(got, after, out):
    chips = got.shape[0] // 24
    state = jnp.zeros((8, HD), F32)
    for j in range(chips):
        out[16 * j : 16 * j + 8, :] = state
        state = got[24 * j : 24 * j + 8, :] + (1.0 - got[24 * j + 16 : 24 * j + 24, :]) * state
    state = jnp.zeros((8, HD), F32)
    for j in reversed(range(chips)):
        out[16 * j + 8 : 16 * j + 16, :] = state
        state = got[24 * j + 8 : 24 * j + 16, :] + (1.0 - got[24 * j + 16 : 24 * j + 24, :]) * state


def scan(got, after):
    chips = got.shape[0] // 24
    return pl.pallas_call(
        scan_kernel,
        in_specs=[whole(), pl.BlockSpec(memory_space=pl.ANY)],
        out_specs=whole(),
        out_shape=jax.ShapeDtypeStruct((chips * 16, HD), F32),
        compiler_params=params(8),
        cost_estimate=cost(got.size * 2, got.size * 8),
        name="scan",
    )(got, after)


def pairs_kernel(q, k, v, g, e, dq, dk, dv, gm, vm, km, mask, gates):
    @pl.when(pl.program_id(0) == 0)
    def _():
        ends = e[...].astype(F32)
        n = ends.shape[1]
        row = lax.broadcasted_iota(jnp.int32, (n, n), 0)
        col = lax.broadcasted_iota(jnp.int32, (n, n), 1)
        before = ends_before(ends)
        below = (row < col).astype(BF16)
        along = nn(jnp.broadcast_to(ends, (8, n)).astype(BF16), below)[:1, :]
        mask[...] = ((col <= row) & (before == along)).astype(F32)
        total = jnp.sum(ends, axis=1, keepdims=True)
        gates[:, :HD] = jnp.broadcast_to((before == 0.0).astype(F32), (n, HD))
        gates[:, HD:] = jnp.broadcast_to((total == before).astype(F32), (n, HD))

    keep = mask[...] > 0.0
    qb, kb, vb, gb = q[...], k[...], v[...], g[...]
    p = jnp.where(keep, nt(gb, vb), 0.0).astype(BF16)
    r = jnp.where(keep, nt(qb, kb), 0.0).astype(BF16)
    dq[...] = nn(p, kb)
    dk[...] = tn(p, qb)
    dv[...] = tn(r, gb)
    opened, closed = gates[:, :HD], gates[:, HD:]
    gm[...] = (gb.astype(F32) * opened).astype(BF16)
    vm[...] = (vb.astype(F32) * closed).astype(BF16)
    km[...] = (kb.astype(F32) * closed).astype(BF16)


def pairs(q, k, v, g, ends):
    rows, cols = q.shape
    head = pl.BlockSpec((rows, HD), lambda h: (0, h))
    out = jax.ShapeDtypeStruct((rows, cols), F32)
    return pl.pallas_call(
        pairs_kernel,
        grid=(cols // HD,),
        in_specs=[head] * 4 + [pl.BlockSpec((1, rows), lambda h: (0, 0))],
        out_specs=[head] * 6,
        out_shape=[out] * 3 + [jax.ShapeDtypeStruct((rows, cols), BF16)] * 3,
        scratch_shapes=[VM((rows, rows), F32), VM((rows, 2 * HD), F32)],
        compiler_params=params(62),
        cost_estimate=cost(10 * rows * rows * cols, 20 * rows * cols),
        name="pairs",
    )(q, k, v, g, ends)


def hidden(dq, dk, dv, gm, vm, km, a_in, b_in):
    outs = ([], [], [])
    for h in range(dq.shape[1] // HD):
        at = slice(h * HD, (h + 1) * HD)
        terms = (
            dq[:, at] + nn(gm[:, at], a_in[at, :]),
            dk[:, at] + nn(vm[:, at], b_in[at, :]),
            dv[:, at] + nt(km[:, at], b_in[at, :]),
        )
        for held, term in zip(outs, terms):
            held.append((term * (1.0 / HD)).astype(BF16))
    return [jnp.concatenate(held, 1) for held in outs]


def fetch(offsets, products, masked, weights, pf, mf, ws, sems, w_sems):
    shards = lax.axis_size("tp")
    me = lax.axis_index("tp")
    count = products[0].shape[0] // shards
    copies = []
    for n, offset in enumerate(offsets):
        start = pl.multiple_of(lax.rem(me + offset, shards) * count, count)
        to = pl.ds(n * count, count)
        for i in range(3):
            copies.append(
                pltpu.make_async_copy(products[i].at[pl.ds(start, count)], pf.at[i, to], sems.at[n, i])
            )
            copies.append(
                pltpu.make_async_copy(masked[i].at[pl.ds(start, count)], mf.at[i, to], sems.at[n, 3 + i])
            )
    loads = [pltpu.make_async_copy(w, ws.at[i], w_sems.at[i]) for i, w in enumerate(weights)]
    for copy in copies + loads:
        copy.start()
    return copies, loads


def finish(copies, loads, pf, mf, ws, a_in, b_in):
    for copy in copies:
        copy.wait()
    parts = hidden(pf.at[0], pf.at[1], pf.at[2], mf.at[0], mf.at[1], mf.at[2], a_in, b_in)
    total = None
    for i, load in enumerate(loads):
        load.wait()
        term = nt(parts[i], ws[i])
        total = term if i == 0 else total + term
    return total


def row_scratch(count, chunks, weights):
    width, cols = weights[0].shape
    dma = pltpu.SemaphoreType.DMA
    return [
        VM((3, chunks * count, cols), F32),
        VM((3, chunks * count, cols), BF16),
        VM((3, width, cols), BF16),
        dma((chunks, 6)),
        dma((3,)),
    ]


def far_kernel(mine, theirs, other, dq, dk, dv, gm, vm, km, wq, wk, wv, low, high, a_in, b_in, *scratch):
    offset = lax.axis_size("tp") // 2
    copies, loads = fetch((offset,), (dq, dk, dv), (gm, vm, km), (wq, wk, wv), *scratch)
    core = lax.rem(lax.axis_index("ctx"), 2)
    is_one = core.astype(F32)
    is_zero = 1.0 - is_one
    half = mine.shape[0] // 2
    rows = 2 * half
    r = other[2 * rows : 2 * rows + 1, :]
    left_a = 1.0 - is_one * r
    left_b = 1.0 - is_zero * r
    own = mine[...].reshape(half // 8, 16, HD)
    far = theirs[...].reshape(half // 8, 16, HD)
    first = core == 0
    for p in range(2):
        pre = jnp.where(first, own, far) if p == 0 else jnp.where(first, far, own)
        at = slice(p * half, (p + 1) * half)
        a = pre[:, :8, :].reshape(half, HD)
        b = pre[:, 8:, :].reshape(half, HD)
        a_in[at, :] = (is_one * other[at, :] + left_a * a).astype(BF16)
        b_in[at, :] = (is_zero * other[rows + p * half : rows + (p + 1) * half, :] + left_b * b).astype(BF16)
    total = finish(copies, loads, *scratch[:3], a_in, b_in)
    split = total.shape[0] // 2
    low[...] = total[:split]
    high[...] = total[split:]


def near_kernel(a_in, b_in, dq, dk, dv, gm, vm, km, wq, wk, wv, up_low, up_high, down_low, down_high, own, *scratch):
    shards = lax.axis_size("tp")
    copies, loads = fetch((1, shards - 1, 0), (dq, dk, dv), (gm, vm, km), (wq, wk, wv), *scratch)
    count = dq.shape[0] // shards
    split = count // 2
    total = finish(copies, loads, *scratch[:3], a_in, b_in)
    up_low[...] = total[:split]
    up_high[...] = total[split:count]
    down_low[...] = total[count : count + split]
    down_high[...] = total[count + split : 2 * count]
    own[...] = total[2 * count :]


def body(tokens_in, w_query, w_key, w_value, grad_out, trajectory_ends):
    row_count, width = tokens_in.shape
    cols = w_query.shape[1]
    shards = lax.axis_size("tp")
    devices = lax.axis_size("ctx")
    ends = trajectory_ends.reshape(1, row_count)
    partner = [(i, i ^ 1) for i in range(devices)]
    groups = [[2 * j + c for j in range(devices // 2)] for c in range(2)]

    def transpose(a):
        unit = a.shape[0] * 2 // devices
        blocks = a.reshape(devices // 2, unit, HD)
        return lax.all_to_all(blocks, "ctx", 0, 0, axis_index_groups=groups, tiled=True).reshape(a.shape)

    q, k, v, message = project(tokens_in, w_query, w_key, w_value, grad_out, ends)
    other = lax.ppermute(message, "ctx", partner)
    got = transpose(fold(message, other))
    dq, dk, dv, gm, vm, km = pairs(q, k, v, grad_out, ends)
    mine = transpose(scan(got, dq))
    theirs = lax.ppermute(mine, "ctx", partner)

    count = row_count // shards
    split = count // 2
    piece = jax.ShapeDtypeStruct((split, width), F32)
    state = jax.ShapeDtypeStruct((cols, HD), BF16)
    weights = (w_query, w_key, w_value)
    away = pl.BlockSpec(memory_space=pl.ANY)
    far_low, far_high, a_in, b_in = pl.pallas_call(
        far_kernel,
        in_specs=[whole()] * 3 + [away] * 9,
        out_specs=[whole()] * 4,
        out_shape=[piece, piece, state, state],
        scratch_shapes=row_scratch(count, 1, weights),
        compiler_params=params(62),
        cost_estimate=cost(6 * count * width * cols, 6 * width * cols),
        name="far",
    )(mine, theirs, other, dq, dk, dv, gm, vm, km, *weights)
    up, down = ring(shards, 1), ring(shards, -1)
    far_up = lax.ppermute(far_low, "tp", up)
    far_down = lax.ppermute(far_high, "tp", down)
    up_low, up_high, down_low, down_high, own = pl.pallas_call(
        near_kernel,
        in_specs=[whole()] * 2 + [away] * 9,
        out_specs=[whole()] * 5,
        out_shape=[piece] * 4 + [jax.ShapeDtypeStruct((count, width), F32)],
        scratch_shapes=row_scratch(count, shards - 1, weights),
        compiler_params=params(56),
        cost_estimate=cost(18 * count * width * cols, 6 * width * cols),
        name="near",
    )(a_in, b_in, dq, dk, dv, gm, vm, km, *weights)
    near_up = lax.ppermute(up_high, "tp", up)
    near_down = lax.ppermute(down_low, "tp", down)
    last_up = lax.ppermute(up_low + far_up, "tp", up)
    last_down = lax.ppermute(down_high + far_down, "tp", down)
    low = own[:split] + near_down + last_up
    top = own[split:] + near_up + last_down
    return jnp.concatenate([low, top], 0).astype(BF16)


def solution(mesh):
    return jax.shard_map(
        body,
        mesh=mesh,
        in_specs=(
            P("ctx", None),
            P(None, "tp"),
            P(None, "tp"),
            P(None, "tp"),
            P("ctx", "tp"),
            P("ctx"),
        ),
        out_specs=P(("ctx", "tp"), None),
        check_vma=False,
    )
```

```python
import jax
import jax.numpy as jnp
from jax import lax
from jax.experimental import pallas as pl
from jax.experimental.pallas import tpu as pltpu
from jax.sharding import PartitionSpec as P

HD = 128
F32 = jnp.float32
BF16 = jnp.bfloat16
MIB = 1 << 20
NT = (((1,), (1,)), ((), ()))
TN = (((0,), (0,)), ((), ()))
VM = pltpu.VMEM


def hbm(a):
    return pltpu.with_memory_space_constraint(a, pltpu.HBM)


def whole():
    return pl.BlockSpec(memory_space=pltpu.VMEM)


def params(mib, **more):
    return pltpu.CompilerParams(vmem_limit_bytes=mib * MIB, **more)


def cost(flops, moved):
    return pl.CostEstimate(flops=int(flops), bytes_accessed=int(moved), transcendentals=0)


def ring(count, step):
    return [(i, (i + step) % count) for i in range(count)]


def nt(a, b):
    return lax.dot_general(a, b, NT, preferred_element_type=F32)


def tn(a, b):
    return lax.dot_general(a, b, TN, preferred_element_type=F32)


def nn(a, b):
    return jnp.dot(a, b, preferred_element_type=F32)


def ends_before(ends):
    n = ends.shape[1]
    row = lax.broadcasted_iota(jnp.int32, (n, n), 0)
    col = lax.broadcasted_iota(jnp.int32, (n, n), 1)
    return jnp.sum(jnp.where(col < row, ends, 0.0), axis=1, keepdims=True)


def project_kernel(x, wq, wk, wv, g, e, q, k, v, msg, xs, ws, gs, acc, stage, in_sem, g_sem, out_sem):
    deep = xs.shape[2]
    steps = xs.shape[0]
    cols = acc.shape[1] // 3
    heads = cols // HD

    def loads(step):
        at = pl.ds(step * deep, deep)
        pairs = [(x.at[:, at], xs.at[step])]
        pairs += [(w.at[at, :], ws.at[step, :, pl.ds(i * cols, cols)]) for i, w in enumerate((wq, wk, wv))]
        return [pltpu.make_async_copy(a, b, in_sem.at[step, i]) for i, (a, b) in enumerate(pairs)]

    for step in range(steps):
        for copy in loads(step):
            copy.start()
    grad = pltpu.make_async_copy(g, gs, g_sem)
    grad.start()
    ends = e[...].astype(F32)
    before = ends_before(ends)
    total = jnp.sum(ends, axis=1, keepdims=True)
    opened = (before == 0.0).astype(F32)
    closed = (total == before).astype(F32)
    msg[2 * heads * HD :, :] = jnp.broadcast_to((total > 0.0).astype(F32), (8, HD))
    for step in range(steps):
        for copy in loads(step):
            copy.wait()
        part = nn(xs[step], ws[step])
        if step == 0:
            acc[...] = part
        elif step < steps - 1:
            acc[...] += part
    last = acc[...] + part
    grad.wait()
    saved = []
    for i in (1, 2, 0):
        stage[i] = last[:, i * cols : (i + 1) * cols].astype(BF16)
        copy = pltpu.make_async_copy(stage.at[i], (q, k, v)[i], out_sem.at[i])
        copy.start()
        saved.append(copy)
    for h in range(heads):
        at = slice(h * HD, (h + 1) * HD)
        vmb = (stage[2, :, at].astype(F32) * closed).astype(BF16)
        msg[at, :] = tn(vmb, stage[1, :, at])
        gmb = (gs[:, at].astype(F32) * opened).astype(BF16)
        msg[(heads + h) * HD : (heads + h + 1) * HD, :] = tn(gmb, stage[0, :, at])
    for copy in saved:
        copy.wait()


def project(x, wq, wk, wv, g, ends):
    rows, width = x.shape
    cols = wq.shape[1]
    steps = 4
    deep = width // steps
    away = pl.BlockSpec(memory_space=pltpu.HBM)
    out = jax.ShapeDtypeStruct((rows, cols), BF16)
    dma = pltpu.SemaphoreType.DMA
    return pl.pallas_call(
        project_kernel,
        in_specs=[away] * 5 + [whole()],
        out_specs=[away] * 3 + [whole()],
        out_shape=[pltpu.HBM((rows, cols), BF16)] * 3 + [jax.ShapeDtypeStruct((2 * cols + 8, HD), F32)],
        scratch_shapes=[
            VM((steps, rows, deep), BF16),
            VM((steps, deep, 3 * cols), BF16),
            VM((rows, cols), BF16),
            VM((rows, 3 * cols), F32),
            VM((3, rows, cols), BF16),
            dma((steps, 4)),
            dma,
            dma((3,)),
        ],
        compiler_params=params(40),
        cost_estimate=cost(6 * rows * width * cols, 2 * (rows * width + 3 * width * cols)),
        name="project",
    )(hbm(x), hbm(wq), hbm(wk), hbm(wv), hbm(g), ends)


def fold_kernel(mine, other, out):
    core = lax.rem(lax.axis_index("ctx"), 2)
    rows = (mine.shape[0] - 8) // 2
    half = rows // 2
    chips = half // 8
    unit = out.shape[0] // chips
    own_r = mine[2 * rows : 2 * rows + 1, :]
    far_r = other[2 * rows : 2 * rows + 1, :]
    is_one = core.astype(F32)
    is_zero = 1.0 - is_one
    own_a = 1.0 - is_zero * far_r
    far_a = 1.0 - is_one * own_r
    own_b = 1.0 - is_one * far_r
    far_b = 1.0 - is_zero * own_r
    flag = jnp.maximum(own_r, far_r)
    base = pl.multiple_of(core * half, 8)
    for j in range(chips):
        a = pl.ds(base + 8 * j, 8)
        b = pl.ds(base + rows + 8 * j, 8)
        out[unit * j : unit * j + 8, 0, :] = own_a * mine[a, :] + far_a * other[a, :]
        out[unit * j + 8 : unit * j + 16, 0, :] = own_b * mine[b, :] + far_b * other[b, :]
        out[unit * j + 16, :, :] = flag


def fold(mine, other):
    half = (mine.shape[0] - 8) // 4
    return pl.pallas_call(
        fold_kernel,
        in_specs=[whole(), whole()],
        out_specs=whole(),
        out_shape=jax.ShapeDtypeStruct((half // 8 * 17, 1, HD), F32),
        compiler_params=params(8),
        cost_estimate=cost(half * HD * 8, mine.size * 8),
        name="fold",
    )(mine, other)


def scan_kernel(got, after, out):
    chips = got.shape[0] // 17
    state = jnp.zeros((8, HD), F32)
    for j in range(chips):
        out[16 * j : 16 * j + 8, :] = state
        state = got[17 * j : 17 * j + 8, 0, :] + (1.0 - got[17 * j + 16, :, :]) * state
    state = jnp.zeros((8, HD), F32)
    for j in reversed(range(chips)):
        out[16 * j + 8 : 16 * j + 16, :] = state
        state = got[17 * j + 8 : 17 * j + 16, 0, :] + (1.0 - got[17 * j + 16, :, :]) * state


def scan(got, after):
    chips = got.shape[0] // 17
    return pl.pallas_call(
        scan_kernel,
        in_specs=[whole(), pl.BlockSpec(memory_space=pltpu.HBM)],
        out_specs=whole(),
        out_shape=jax.ShapeDtypeStruct((chips * 16, HD), F32),
        compiler_params=params(8),
        cost_estimate=cost(got.size * 2, got.size * 8),
        name="scan",
    )(got, hbm(after))


def pairs_kernel(q, k, v, g, e, dq, dk, dv, gm, vm, km, token, mask, gates):
    @pl.when(pl.program_id(0) == 0)
    def _():
        ends = e[...].astype(F32)
        n = ends.shape[1]
        row = lax.broadcasted_iota(jnp.int32, (n, n), 0)
        col = lax.broadcasted_iota(jnp.int32, (n, n), 1)
        before = ends_before(ends)
        below = (row < col).astype(BF16)
        along = nn(jnp.broadcast_to(ends, (8, n)).astype(BF16), below)[:1, :]
        mask[...] = ((col <= row) & (before == along)).astype(F32)
        total = jnp.sum(ends, axis=1, keepdims=True)
        gates[:, :HD] = jnp.broadcast_to((before == 0.0).astype(F32), (n, HD))
        gates[:, HD:] = jnp.broadcast_to((total == before).astype(F32), (n, HD))

    keep = mask[...] > 0.0
    qb, kb, vb, gb = q[...], k[...], v[...], g[...]
    p = jnp.where(keep, nt(gb, vb), 0.0).astype(BF16)
    r = jnp.where(keep, nt(qb, kb), 0.0).astype(BF16)
    dq[...] = nn(p, kb)
    dk[...] = tn(p, qb)
    dv[...] = tn(r, gb)
    opened, closed = gates[:, :HD], gates[:, HD:]
    gm[...] = (gb.astype(F32) * opened).astype(BF16)
    vm[...] = (vb.astype(F32) * closed).astype(BF16)
    km[...] = (kb.astype(F32) * closed).astype(BF16)
    token[...] = closed[:8]


def pairs(q, k, v, g, ends):
    rows, cols = q.shape
    head = pl.BlockSpec((rows, HD), lambda h: (0, h))
    out = jax.ShapeDtypeStruct((rows, cols), F32)
    return pl.pallas_call(
        pairs_kernel,
        grid=(cols // HD,),
        in_specs=[head] * 4 + [pl.BlockSpec((1, rows), lambda h: (0, 0))],
        out_specs=[head] * 6 + [pl.BlockSpec((8, HD), lambda h: (0, 0))],
        out_shape=[out] * 3
        + [jax.ShapeDtypeStruct((rows, cols), BF16)] * 3
        + [jax.ShapeDtypeStruct((8, HD), F32)],
        scratch_shapes=[VM((rows, rows), F32), VM((rows, 2 * HD), F32)],
        compiler_params=params(62),
        cost_estimate=cost(10 * rows * rows * cols, 20 * rows * cols),
        name="pairs",
    )(q, k, v, g, ends)


def hidden(dq, dk, dv, gm, vm, km, a_in, b_in):
    outs = ([], [], [])
    for h in range(dq.shape[1] // HD):
        at = slice(h * HD, (h + 1) * HD)
        terms = (
            dq[:, at] + nn(gm[:, at], a_in[at, :]),
            dk[:, at] + nn(vm[:, at], b_in[at, :]),
            dv[:, at] + nt(km[:, at], b_in[at, :]),
        )
        for held, term in zip(outs, terms):
            held.append((term * (1.0 / HD)).astype(BF16))
    return [jnp.concatenate(held, 1) for held in outs]


def fetch(pieces, products, masked, pf, mf, sems):
    shards = lax.axis_size("tp")
    me = lax.axis_index("tp")
    count = products[0].shape[0] // shards
    copies = []
    base = 0
    for n, (offset, begin, size) in enumerate(pieces):
        start = pl.multiple_of(lax.rem(me + offset, shards) * count + begin, size)
        to = pl.ds(base, size)
        base += size
        for i in range(3):
            copies.append(pltpu.make_async_copy(products[i].at[pl.ds(start, size)], pf.at[i, to], sems.at[n, i]))
            copies.append(pltpu.make_async_copy(masked[i].at[pl.ds(start, size)], mf.at[i, to], sems.at[n, 3 + i]))
    for copy in copies:
        copy.start()
    return copies


def finish(parts, weights, n, step):
    at = slice(n * step, (n + 1) * step)
    total = nt(parts[0], weights[0][at, :])
    for part, weight in zip(parts[1:], weights[1:]):
        total = total + nt(part, weight[at, :])
    return total


def row_scratch(rows, pieces, cols):
    return [
        VM((3, rows, cols), F32),
        VM((3, rows, cols), BF16),
        pltpu.SemaphoreType.DMA((pieces, 6)),
    ]


def pull(weights, held, base, sems):
    steps = sems.shape[0]
    step = held[0].shape[0] // steps
    loads = []
    for n in range(steps):
        to = pl.ds(n * step, step)
        for i, (w, h) in enumerate(zip(weights, held)):
            load = pltpu.make_async_copy(w.at[pl.ds(base + n * step, step), :], h.at[to, :], sems.at[n, i])
            load.start()
            loads.append(load)
    return loads


def multiply(parts, held, loads, low, high):
    split = low.shape[0]
    step = 3 * held[0].shape[0] // len(loads)
    for n in range(len(loads) // 3):
        for load in loads[3 * n : 3 * n + 3]:
            load.wait()
        total = finish(parts, held, n, step)
        at = slice(n * step, (n + 1) * step)
        low[:, at] = total[:split]
        high[:, at] = total[split:]


def far_kernel(
    mine, theirs, other, dq, dk, dv, gm, vm, km, wq, wk, wv, low, high, a_in, b_in, hq, hk, hv, hid, pf, mf, sems, w_sems
):
    copies = fetch(((lax.axis_size("tp") // 2, 0, 2 * low.shape[0]),), (dq, dk, dv), (gm, vm, km), pf, mf, sems)
    loads = pull((wq, wk, wv), (hq, hk, hv), 0, w_sems)
    core = lax.rem(lax.axis_index("ctx"), 2)
    is_one = core.astype(F32)
    is_zero = 1.0 - is_one
    half = mine.shape[0] // 2
    rows = 2 * half
    r = other[2 * rows : 2 * rows + 1, :]
    left_a = 1.0 - is_one * r
    left_b = 1.0 - is_zero * r
    own = mine[...].reshape(half // 8, 16, HD)
    far = theirs[...].reshape(half // 8, 16, HD)
    first = core == 0
    for p in range(2):
        pre = jnp.where(first, own, far) if p == 0 else jnp.where(first, far, own)
        at = slice(p * half, (p + 1) * half)
        a = pre[:, :8, :].reshape(half, HD)
        b = pre[:, 8:, :].reshape(half, HD)
        a_in[at, :] = (is_one * other[at, :] + left_a * a).astype(BF16)
        b_in[at, :] = (is_zero * other[rows + p * half : rows + (p + 1) * half, :] + left_b * b).astype(BF16)
    for copy in copies:
        copy.wait()
    parts = hidden(*(pf.at[i] for i in range(3)), *(mf.at[i] for i in range(3)), a_in, b_in)
    for i in range(3):
        hid[i] = parts[i]
    multiply(parts, (hq, hk, hv), loads, low, high)


def rest_kernel(hid, wq, wk, wv, low, high, hq, hk, hv, w_sems):
    loads = pull((wq, wk, wv), (hq, hk, hv), hq.shape[0], w_sems)
    multiply([hid[i] for i in range(3)], (hq, hk, hv), loads, low, high)


def near_parts(pieces, a_in, b_in, products, masked, pf, mf, sems):
    for copy in fetch(pieces, products, masked, pf, mf, sems):
        copy.wait()
    return hidden(*(pf.at[i] for i in range(3)), *(mf.at[i] for i in range(3)), a_in, b_in)


def slabs(parts, first, second, step=512):
    half = first[0].shape[0]
    for n in range(2 * half // step):
        side, inner = divmod(n, half // step)
        yield side, slice(n * step, (n + 1) * step), slice(inner * step, (inner + 1) * step), finish(
            parts, (first, second)[side], inner, step
        )


def near_kernel(a_in, b_in, dq, dk, dv, gm, vm, km, hq, hk, hv, rq, rk, rv, up_high, down_low, pf, mf, sems):
    last = lax.axis_size("tp") - 1
    split = up_high.shape[0]
    pieces = ((1, split, split), (last, 0, split))
    parts = near_parts(pieces, a_in, b_in, (dq, dk, dv), (gm, vm, km), pf, mf, sems)
    for _, at, _, total in slabs(parts, (hq, hk, hv), (rq, rk, rv)):
        up_high[:, at] = total[:split]
        down_low[:, at] = total[split:]


def last_kernel(
    a_in, b_in, dq, dk, dv, gm, vm, km, hq, hk, hv, rq, rk, rv, after0, after1, ul0, ul1, dh0, dh1, own, pf, mf, sems
):
    last = lax.axis_size("tp") - 1
    split = ul0.shape[0]
    pieces = ((1, 0, split), (last, split, split), (0, 0, 2 * split))
    parts = near_parts(pieces, a_in, b_in, (dq, dk, dv), (gm, vm, km), pf, mf, sems)
    for side, at, within, total in slabs(parts, (hq, hk, hv), (rq, rk, rv)):
        (ul0, ul1)[side][:, within] = total[:split]
        (dh0, dh1)[side][:, within] = total[split : 2 * split]
        own[:, at] = total[2 * split :]


def join_kernel(own, near_down, near_up, lu0, lu1, ld0, ld1, out):
    split, half = lu0.shape
    for side in range(2):
        at = slice(side * half, (side + 1) * half)
        low = own[:split, at] + near_down[:, at] + (lu0, lu1)[side][...]
        top = own[split:, at] + near_up[:, at] + (ld0, ld1)[side][...]
        out[:split, at] = low.astype(BF16)
        out[split:, at] = top.astype(BF16)


def body(tokens_in, w_query, w_key, w_value, grad_out, trajectory_ends):
    row_count, width = tokens_in.shape
    cols = w_query.shape[1]
    shards = lax.axis_size("tp")
    devices = lax.axis_size("ctx")
    ends = trajectory_ends.reshape(1, row_count)
    partner = [(i, i ^ 1) for i in range(devices)]
    groups = [[2 * j + c for j in range(devices // 2)] for c in range(2)]

    def transpose(a):
        unit = a.shape[0] * 2 // devices
        blocks = a.reshape(devices // 2, unit, *a.shape[1:])
        return lax.all_to_all(blocks, "ctx", 0, 0, axis_index_groups=groups, tiled=True).reshape(a.shape)

    q, k, v, message = project(tokens_in, w_query, w_key, w_value, grad_out, ends)
    other = lax.ppermute(message, "ctx", partner)
    got = transpose(fold(message, other))
    dq, dk, dv, gm, vm, km, token = pairs(q, k, v, grad_out, ends)
    mine = transpose(scan(got, token))
    theirs = lax.ppermute(mine, "ctx", partner)

    count = row_count // shards
    split = count // 2
    piece = jax.ShapeDtypeStruct((split, width), F32)
    state = jax.ShapeDtypeStruct((cols, HD), BF16)
    weights = (w_query, w_key, w_value)
    away = pl.BlockSpec(memory_space=pltpu.HBM)
    half = width // 2
    weight = jax.ShapeDtypeStruct((half, cols), BF16)
    part = jax.ShapeDtypeStruct((split, half), F32)
    hid_shape = jax.ShapeDtypeStruct((3, count, cols), BF16)
    rows = tuple(hbm(a) for a in (dq, dk, dv, gm, vm, km))
    fixed = tuple(hbm(w) for w in weights)
    up, down = ring(shards, 1), ring(shards, -1)
    w_sems = pltpu.SemaphoreType.DMA((2, 3))
    low0, high0, a_in, b_in, *held0, hid = pl.pallas_call(
        far_kernel,
        in_specs=[whole()] * 3 + [away] * 9,
        out_specs=[whole()] * 8,
        out_shape=[part, part, state, state] + [weight] * 3 + [hid_shape],
        scratch_shapes=row_scratch(count, 1, cols) + [w_sems],
        compiler_params=params(16),
        cost_estimate=cost(3 * count * width * cols, 3 * width * cols),
        name="far",
    )(mine, theirs, other, *rows, *fixed)
    far_up0 = lax.ppermute(low0, "tp", up)
    far_down0 = lax.ppermute(high0, "tp", down)
    low1, high1, *held1 = pl.pallas_call(
        rest_kernel,
        in_specs=[whole()] + [away] * 3,
        out_specs=[whole()] * 5,
        out_shape=[part, part] + [weight] * 3,
        scratch_shapes=[w_sems],
        compiler_params=params(16),
        cost_estimate=cost(3 * count * width * cols, 3 * width * cols),
        name="rest",
    )(hid, *fixed)
    far_up1 = lax.ppermute(low1, "tp", up)
    far_down1 = lax.ppermute(high1, "tp", down)
    up_high, down_low = pl.pallas_call(
        near_kernel,
        in_specs=[whole()] * 2 + [away] * 6 + [whole()] * 6,
        out_specs=[whole()] * 2,
        out_shape=[piece] * 2,
        scratch_shapes=row_scratch(count, 2, cols),
        compiler_params=params(16),
        cost_estimate=cost(6 * count * width * cols, 6 * width * cols),
        name="near",
    )(a_in, b_in, *rows, *held0, *held1)
    near_up = lax.ppermute(up_high, "tp", up)
    near_down = lax.ppermute(down_low, "tp", down)
    ul0, ul1, dh0, dh1, own = pl.pallas_call(
        last_kernel,
        in_specs=[whole()] * 2 + [away] * 6 + [whole()] * 6 + [pl.BlockSpec(memory_space=pl.ANY)] * 2,
        out_specs=[whole()] * 5,
        out_shape=[part] * 4 + [jax.ShapeDtypeStruct((count, width), F32)],
        scratch_shapes=row_scratch(2 * count, 3, cols),
        compiler_params=params(20),
        cost_estimate=cost(12 * count * width * cols, 6 * width * cols),
        name="last",
    )(a_in, b_in, *rows, *held0, *held1, up_high, down_low)
    last_up0 = lax.ppermute(ul0 + far_up0, "tp", up)
    last_down0 = lax.ppermute(dh0 + far_down0, "tp", down)
    last_up1 = lax.ppermute(ul1 + far_up1, "tp", up)
    last_down1 = lax.ppermute(dh1 + far_down1, "tp", down)
    return pl.pallas_call(
        join_kernel,
        in_specs=[whole()] * 7,
        out_specs=whole(),
        out_shape=jax.ShapeDtypeStruct((count, width), BF16),
        compiler_params=params(12),
        name="join",
    )(own, near_down, near_up, last_up0, last_up1, last_down0, last_down1)


def solution(mesh):
    return jax.shard_map(
        body,
        mesh=mesh,
        in_specs=(
            P("ctx", None),
            P(None, "tp"),
            P(None, "tp"),
            P(None, "tp"),
            P("ctx", "tp"),
            P("ctx"),
        ),
        out_specs=P(("ctx", "tp"), None),
        check_vma=False,
    )
```

```python
import jax
import jax.numpy as jnp
from jax import lax
from jax.experimental import pallas as pl
from jax.experimental.pallas import tpu as pltpu
from jax.sharding import PartitionSpec as P

HD = 128
F32 = jnp.float32
BF16 = jnp.bfloat16
MIB = 1 << 20
NT = (((1,), (1,)), ((), ()))
TN = (((0,), (0,)), ((), ()))
VM = pltpu.VMEM


def hbm(a):
    return pltpu.with_memory_space_constraint(a, pltpu.HBM)


def whole():
    return pl.BlockSpec(memory_space=pltpu.VMEM)


def params(mib, **more):
    return pltpu.CompilerParams(vmem_limit_bytes=mib * MIB, **more)


def cost(flops, moved):
    return pl.CostEstimate(flops=int(flops), bytes_accessed=int(moved), transcendentals=0)


def ring(count, step):
    return [(i, (i + step) % count) for i in range(count)]


def nt(a, b):
    return lax.dot_general(a, b, NT, preferred_element_type=F32)


def tn(a, b):
    return lax.dot_general(a, b, TN, preferred_element_type=F32)


def nn(a, b):
    return jnp.dot(a, b, preferred_element_type=F32)


def ends_before(ends):
    n = ends.shape[1]
    row = lax.broadcasted_iota(jnp.int32, (n, n), 0)
    col = lax.broadcasted_iota(jnp.int32, (n, n), 1)
    return jnp.sum(jnp.where(col < row, ends, 0.0), axis=1, keepdims=True)


def project_kernel(x, wq, wk, wv, g, e, q, k, v, msg, xs, ws, gs, acc, stage, es, in_sem, g_sem, out_sem, e_sem):
    deep = xs.shape[2]
    steps = xs.shape[0]
    cols = acc.shape[1] // 3
    heads = cols // HD

    def loads(step):
        at = pl.ds(step * deep, deep)
        pairs = [(x.at[:, at], xs.at[step])]
        pairs += [(w.at[at, :], ws.at[step, :, pl.ds(i * cols, cols)]) for i, w in enumerate((wq, wk, wv))]
        return [pltpu.make_async_copy(a, b, in_sem.at[step, i]) for i, (a, b) in enumerate(pairs)]

    for step in range(steps):
        for copy in loads(step):
            copy.start()
    grad = pltpu.make_async_copy(g, gs, g_sem)
    grad.start()
    flags = pltpu.make_async_copy(e, es, e_sem)
    flags.start()
    for step in range(steps):
        for copy in loads(step):
            copy.wait()
        part = nn(xs[step], ws[step])
        if step == 0:
            acc[...] = part
        elif step < steps - 1:
            acc[...] += part
        if step == 1:
            flags.wait()
            ends = es[...].astype(F32)
            before = ends_before(ends)
            total = jnp.sum(ends, axis=1, keepdims=True)
            opened = (before == 0.0).astype(F32)
            closed = (total == before).astype(F32)
            msg[2 * heads * HD :, :] = jnp.broadcast_to((total > 0.0).astype(F32), (8, HD))
    last = acc[...] + part
    grad.wait()
    saved = []
    for i in (1, 2, 0):
        stage[i] = last[:, i * cols : (i + 1) * cols].astype(BF16)
        copy = pltpu.make_async_copy(stage.at[i], (q, k, v)[i], out_sem.at[i])
        copy.start()
        saved.append(copy)
    for h in range(heads):
        at = slice(h * HD, (h + 1) * HD)
        vmb = (stage[2, :, at].astype(F32) * closed).astype(BF16)
        msg[at, :] = tn(vmb, stage[1, :, at])
        gmb = (gs[:, at].astype(F32) * opened).astype(BF16)
        msg[(heads + h) * HD : (heads + h + 1) * HD, :] = tn(gmb, stage[0, :, at])
    for copy in saved:
        copy.wait()


def project(x, wq, wk, wv, g, ends):
    rows, width = x.shape
    cols = wq.shape[1]
    steps = 4
    deep = width // steps
    away = pl.BlockSpec(memory_space=pltpu.HBM)
    out = jax.ShapeDtypeStruct((rows, cols), BF16)
    dma = pltpu.SemaphoreType.DMA
    return pl.pallas_call(
        project_kernel,
        in_specs=[away] * 6,
        out_specs=[away] * 3 + [whole()],
        out_shape=[pltpu.HBM((rows, cols), BF16)] * 3 + [jax.ShapeDtypeStruct((2 * cols + 8, HD), F32)],
        scratch_shapes=[
            VM((steps, rows, deep), BF16),
            VM((steps, deep, 3 * cols), BF16),
            VM((rows, cols), BF16),
            VM((rows, 3 * cols), F32),
            VM((3, rows, cols), BF16),
            VM((1, rows), jnp.int32),
            dma((steps, 4)),
            dma,
            dma((3,)),
            dma,
        ],
        compiler_params=params(40),
        cost_estimate=cost(6 * rows * width * cols, 2 * (rows * width + 3 * width * cols)),
        name="project",
    )(hbm(x), hbm(wq), hbm(wk), hbm(wv), hbm(g), hbm(ends))


def fold_kernel(mine, other, out):
    core = lax.rem(lax.axis_index("ctx"), 2)
    rows = (mine.shape[0] - 8) // 2
    half = rows // 2
    chips = half // 8
    unit = out.shape[0] // chips
    own_r = mine[2 * rows : 2 * rows + 1, :]
    far_r = other[2 * rows : 2 * rows + 1, :]
    is_one = core.astype(F32)
    is_zero = 1.0 - is_one
    own_a = 1.0 - is_zero * far_r
    far_a = 1.0 - is_one * own_r
    own_b = 1.0 - is_one * far_r
    far_b = 1.0 - is_zero * own_r
    flag = jnp.maximum(own_r, far_r)
    base = pl.multiple_of(core * half, 8)
    for j in range(chips):
        a = pl.ds(base + 8 * j, 8)
        b = pl.ds(base + rows + 8 * j, 8)
        out[unit * j : unit * j + 8, 0, :] = own_a * mine[a, :] + far_a * other[a, :]
        out[unit * j + 8 : unit * j + 16, 0, :] = own_b * mine[b, :] + far_b * other[b, :]
        out[unit * j + 16, :, :] = flag


def fold(mine, other):
    half = (mine.shape[0] - 8) // 4
    return pl.pallas_call(
        fold_kernel,
        in_specs=[whole(), whole()],
        out_specs=whole(),
        out_shape=jax.ShapeDtypeStruct((half // 8 * 17, 1, HD), F32),
        compiler_params=params(8),
        cost_estimate=cost(half * HD * 8, mine.size * 8),
        name="fold",
    )(mine, other)


def scan_kernel(got, after, out):
    chips = got.shape[0] // 17
    state = jnp.zeros((8, HD), F32)
    for j in range(chips):
        out[16 * j : 16 * j + 8, :] = state
        state = got[17 * j : 17 * j + 8, 0, :] + (1.0 - got[17 * j + 16, :, :]) * state
    state = jnp.zeros((8, HD), F32)
    for j in reversed(range(chips)):
        out[16 * j + 8 : 16 * j + 16, :] = state
        state = got[17 * j + 8 : 17 * j + 16, 0, :] + (1.0 - got[17 * j + 16, :, :]) * state


def scan(got, after):
    chips = got.shape[0] // 17
    return pl.pallas_call(
        scan_kernel,
        in_specs=[whole(), pl.BlockSpec(memory_space=pltpu.HBM)],
        out_specs=whole(),
        out_shape=jax.ShapeDtypeStruct((chips * 16, HD), F32),
        compiler_params=params(8),
        cost_estimate=cost(got.size * 2, got.size * 8),
        name="scan",
    )(got, hbm(after))


def pairs_kernel(q, k, v, g, e, dq, dk, dv, gm, vm, km, token, mask, gates):
    @pl.when(pl.program_id(0) == 0)
    def _():
        ends = e[...].astype(F32)
        n = ends.shape[1]
        row = lax.broadcasted_iota(jnp.int32, (n, n), 0)
        col = lax.broadcasted_iota(jnp.int32, (n, n), 1)
        before = ends_before(ends)
        below = (row < col).astype(BF16)
        along = nn(jnp.broadcast_to(ends, (8, n)).astype(BF16), below)[:1, :]
        mask[...] = ((col <= row) & (before == along)).astype(F32)
        total = jnp.sum(ends, axis=1, keepdims=True)
        gates[:, :HD] = jnp.broadcast_to((before == 0.0).astype(F32), (n, HD))
        gates[:, HD:] = jnp.broadcast_to((total == before).astype(F32), (n, HD))

    keep = mask[...] > 0.0
    qb, kb, vb, gb = q[...], k[...], v[...], g[...]
    p = jnp.where(keep, nt(gb, vb), 0.0).astype(BF16)
    r = jnp.where(keep, nt(qb, kb), 0.0).astype(BF16)
    dq[...] = nn(p, kb)
    dk[...] = tn(p, qb)
    dv[...] = tn(r, gb)
    opened, closed = gates[:, :HD], gates[:, HD:]
    gm[...] = (gb.astype(F32) * opened).astype(BF16)
    vm[...] = (vb.astype(F32) * closed).astype(BF16)
    km[...] = (kb.astype(F32) * closed).astype(BF16)
    token[...] = closed[:8]


def pairs(q, k, v, g, ends):
    rows, cols = q.shape
    head = pl.BlockSpec((rows, HD), lambda h: (0, h))
    out = jax.ShapeDtypeStruct((rows, cols), F32)
    return pl.pallas_call(
        pairs_kernel,
        grid=(cols // HD,),
        in_specs=[head] * 4 + [pl.BlockSpec((1, rows), lambda h: (0, 0))],
        out_specs=[head] * 6 + [pl.BlockSpec((8, HD), lambda h: (0, 0))],
        out_shape=[out] * 3
        + [jax.ShapeDtypeStruct((rows, cols), BF16)] * 3
        + [jax.ShapeDtypeStruct((8, HD), F32)],
        scratch_shapes=[VM((rows, rows), F32), VM((rows, 2 * HD), F32)],
        compiler_params=params(62),
        cost_estimate=cost(10 * rows * rows * cols, 20 * rows * cols),
        name="pairs",
    )(q, k, v, g, ends)


def hidden(dq, dk, dv, gm, vm, km, a_in, b_in):
    outs = ([], [], [])
    for h in range(dq.shape[1] // HD):
        at = slice(h * HD, (h + 1) * HD)
        terms = (
            dq[:, at] + nn(gm[:, at], a_in[at, :]),
            dk[:, at] + nn(vm[:, at], b_in[at, :]),
            dv[:, at] + nt(km[:, at], b_in[at, :]),
        )
        for held, term in zip(outs, terms):
            held.append((term * (1.0 / HD)).astype(BF16))
    return [jnp.concatenate(held, 1) for held in outs]


def fetch(pieces, products, masked, pf, mf, sems):
    shards = lax.axis_size("tp")
    me = lax.axis_index("tp")
    count = products[0].shape[0] // shards
    copies = []
    base = 0
    for n, (offset, begin, size) in enumerate(pieces):
        start = pl.multiple_of(lax.rem(me + offset, shards) * count + begin, size)
        to = pl.ds(base, size)
        base += size
        for i in range(3):
            copies.append(pltpu.make_async_copy(products[i].at[pl.ds(start, size)], pf.at[i, to], sems.at[n, i]))
            copies.append(pltpu.make_async_copy(masked[i].at[pl.ds(start, size)], mf.at[i, to], sems.at[n, 3 + i]))
    for copy in copies:
        copy.start()
    return copies


def finish(parts, weights, n, step):
    at = slice(n * step, (n + 1) * step)
    total = nt(parts[0], weights[0][at, :])
    for part, weight in zip(parts[1:], weights[1:]):
        total = total + nt(part, weight[at, :])
    return total


def row_scratch(rows, pieces, cols):
    return [
        VM((3, rows, cols), F32),
        VM((3, rows, cols), BF16),
        pltpu.SemaphoreType.DMA((pieces, 6)),
    ]


def pull(weights, held, base, sems):
    loads = []
    for i, (w, h) in enumerate(zip(weights, held)):
        load = pltpu.make_async_copy(w.at[pl.ds(base, h.shape[0]), :], h, sems.at[i])
        load.start()
        loads.append(load)
    return loads


def slabs(parts, groups, step=512):
    n = 0
    for group in groups:
        for inner in range(group[0].shape[0] // step):
            yield n // 2, slice(n * step, (n + 1) * step), slice(n % 2 * step, (n % 2 + 1) * step), finish(
                parts, group, inner, step
            )
            n += 1


def warm_kernel(after, dq, dk, dv, gm, vm, km, wq, wk, wv, hq, hk, hv, pf, mf, sems, w_sems):
    piece = (lax.axis_size("tp") // 2, 0, pf.shape[1])
    copies = fetch((piece,), (dq, dk, dv), (gm, vm, km), pf, mf, sems)
    for copy in copies + pull((wq, wk, wv), (hq, hk, hv), 0, w_sems):
        copy.wait()


def far_kernel(
    mine, theirs, other, pf, mf, hq, hk, hv, wq, wk, wv, low, high, a_in, b_in, nq, nk, nv, hid, w_sems
):
    loads = pull((wq, wk, wv), (nq, nk, nv), hq.shape[0], w_sems)
    core = lax.rem(lax.axis_index("ctx"), 2)
    is_one = core.astype(F32)
    is_zero = 1.0 - is_one
    half = mine.shape[0] // 2
    rows = 2 * half
    r = other[2 * rows : 2 * rows + 1, :]
    left_a = 1.0 - is_one * r
    left_b = 1.0 - is_zero * r
    own = mine[...].reshape(half // 8, 16, HD)
    far = theirs[...].reshape(half // 8, 16, HD)
    first = core == 0
    for p in range(2):
        pre = jnp.where(first, own, far) if p == 0 else jnp.where(first, far, own)
        at = slice(p * half, (p + 1) * half)
        a = pre[:, :8, :].reshape(half, HD)
        b = pre[:, 8:, :].reshape(half, HD)
        a_in[at, :] = (is_one * other[at, :] + left_a * a).astype(BF16)
        b_in[at, :] = (is_zero * other[rows + p * half : rows + (p + 1) * half, :] + left_b * b).astype(BF16)
    parts = hidden(*(pf.at[i] for i in range(3)), *(mf.at[i] for i in range(3)), a_in, b_in)
    split = low.shape[0]
    for i in range(3):
        hid[i] = parts[i]
    for _, at, _, total in slabs(parts, ((hq, hk, hv),)):
        low[:, at] = total[:split]
        high[:, at] = total[split:]
    for load in loads:
        load.wait()


def rest_kernel(hid, nq, nk, nv, dq, dk, dv, gm, vm, km, low, high, pf, mf, sems):
    last = lax.axis_size("tp") - 1
    rows = pf.shape[1] // 2
    copies = fetch(((1, rows, rows), (last, 0, rows)), (dq, dk, dv), (gm, vm, km), pf, mf, sems)
    split = low.shape[0]
    for _, at, _, total in slabs([hid[i] for i in range(3)], ((nq, nk, nv),)):
        low[:, at] = total[:split]
        high[:, at] = total[split:]
    for copy in copies:
        copy.wait()


def near_parts(pieces, a_in, b_in, products, masked, pf, mf, sems):
    for copy in fetch(pieces, products, masked, pf, mf, sems):
        copy.wait()
    return hidden(*(pf.at[i] for i in range(3)), *(mf.at[i] for i in range(3)), a_in, b_in)


def near_kernel(a_in, b_in, pf, mf, hq, hk, hv, nq, nk, nv, up_high, down_low):
    split = up_high.shape[0]
    parts = hidden(*(pf.at[i] for i in range(3)), *(mf.at[i] for i in range(3)), a_in, b_in)
    for _, at, _, total in slabs(parts, ((hq, hk, hv), (nq, nk, nv))):
        up_high[:, at] = total[:split]
        down_low[:, at] = total[split:]


def last_kernel(
    a_in, b_in, dq, dk, dv, gm, vm, km, hq, hk, hv, nq, nk, nv, after0, after1, ul0, ul1, dh0, dh1, own, pf, mf, sems
):
    last = lax.axis_size("tp") - 1
    split = ul0.shape[0]
    pieces = ((1, 0, split), (last, split, split), (0, 0, 2 * split))
    parts = near_parts(pieces, a_in, b_in, (dq, dk, dv), (gm, vm, km), pf, mf, sems)
    for side, at, within, total in slabs(parts, ((hq, hk, hv), (nq, nk, nv))):
        (ul0, ul1)[side][:, within] = total[:split]
        (dh0, dh1)[side][:, within] = total[split : 2 * split]
        own[:, at] = total[2 * split :]


def join_kernel(own, near_down, near_up, lu0, lu1, ld0, ld1, out):
    split, half = lu0.shape
    for side in range(2):
        at = slice(side * half, (side + 1) * half)
        low = own[:split, at] + near_down[:, at] + (lu0, lu1)[side][...]
        top = own[split:, at] + near_up[:, at] + (ld0, ld1)[side][...]
        out[:split, at] = low.astype(BF16)
        out[split:, at] = top.astype(BF16)


def body(tokens_in, w_query, w_key, w_value, grad_out, trajectory_ends):
    row_count, width = tokens_in.shape
    cols = w_query.shape[1]
    shards = lax.axis_size("tp")
    devices = lax.axis_size("ctx")
    ends = trajectory_ends.reshape(1, row_count)
    partner = [(i, i ^ 1) for i in range(devices)]
    groups = [[2 * j + c for j in range(devices // 2)] for c in range(2)]

    def transpose(a):
        unit = a.shape[0] * 2 // devices
        blocks = a.reshape(devices // 2, unit, *a.shape[1:])
        return lax.all_to_all(blocks, "ctx", 0, 0, axis_index_groups=groups, tiled=True).reshape(a.shape)

    q, k, v, message = project(tokens_in, w_query, w_key, w_value, grad_out, ends)
    other = lax.ppermute(message, "ctx", partner)
    got = transpose(fold(message, other))
    dq, dk, dv, gm, vm, km, token = pairs(q, k, v, grad_out, ends)
    mine = transpose(scan(got, token))
    theirs = lax.ppermute(mine, "ctx", partner)

    count = row_count // shards
    split = count // 2
    piece = jax.ShapeDtypeStruct((split, width), F32)
    state = jax.ShapeDtypeStruct((cols, HD), BF16)
    weights = (w_query, w_key, w_value)
    away = pl.BlockSpec(memory_space=pltpu.HBM)
    half = width // 2
    part = jax.ShapeDtypeStruct((split, half), F32)
    side = [jax.ShapeDtypeStruct((half, cols), BF16)] * 3
    hid_shape = jax.ShapeDtypeStruct((3, count, cols), BF16)
    rows = tuple(hbm(a) for a in (dq, dk, dv, gm, vm, km))
    fixed = tuple(hbm(w) for w in weights)
    up, down = ring(shards, 1), ring(shards, -1)
    w_sems = pltpu.SemaphoreType.DMA((3,))
    *held0, pf, mf = pl.pallas_call(
        warm_kernel,
        in_specs=[pl.BlockSpec(memory_space=pl.ANY)] + [away] * 9,
        out_specs=[whole()] * 5,
        out_shape=[jax.ShapeDtypeStruct((half, cols), BF16)] * 3
        + [jax.ShapeDtypeStruct((3, count, cols), F32), hid_shape],
        scratch_shapes=[pltpu.SemaphoreType.DMA((1, 6)), w_sems],
        compiler_params=params(4),
        cost_estimate=cost(1, 6 * width * cols),
        name="warm",
    )(mine, *rows, *fixed)
    low0, high0, a_in, b_in, *held1, hid = pl.pallas_call(
        far_kernel,
        in_specs=[whole()] * 8 + [away] * 3,
        out_specs=[whole()] * 8,
        out_shape=[part, part, state, state] + side + [hid_shape],
        scratch_shapes=[w_sems],
        compiler_params=params(16),
        cost_estimate=cost(3 * count * width * cols, 3 * width * cols),
        name="far",
    )(mine, theirs, other, pf, mf, *held0, *fixed)
    far_up0 = lax.ppermute(low0, "tp", up)
    far_down0 = lax.ppermute(high0, "tp", down)
    low1, high1, near_pf, near_mf = pl.pallas_call(
        rest_kernel,
        in_specs=[whole()] * 4 + [away] * 6,
        out_specs=[whole()] * 4,
        out_shape=[part, part, jax.ShapeDtypeStruct((3, count, cols), F32), hid_shape],
        scratch_shapes=[pltpu.SemaphoreType.DMA((2, 6))],
        compiler_params=params(16),
        cost_estimate=cost(3 * count * width * cols, 3 * width * cols),
        name="rest",
    )(hid, *held1, *rows)
    far_up1 = lax.ppermute(low1, "tp", up)
    far_down1 = lax.ppermute(high1, "tp", down)
    up_high, down_low = pl.pallas_call(
        near_kernel,
        in_specs=[whole()] * 10,
        out_specs=[whole()] * 2,
        out_shape=[piece] * 2,
        compiler_params=params(16),
        cost_estimate=cost(6 * count * width * cols, 6 * width * cols),
        name="near",
    )(a_in, b_in, near_pf, near_mf, *held0, *held1)
    near_up = lax.ppermute(up_high, "tp", up)
    near_down = lax.ppermute(down_low, "tp", down)
    ul0, ul1, dh0, dh1, own = pl.pallas_call(
        last_kernel,
        in_specs=[whole()] * 2 + [away] * 6 + [whole()] * 6 + [pl.BlockSpec(memory_space=pl.ANY)] * 2,
        out_specs=[whole()] * 5,
        out_shape=[part] * 4 + [jax.ShapeDtypeStruct((count, width), F32)],
        scratch_shapes=row_scratch(2 * count, 3, cols),
        compiler_params=params(20),
        cost_estimate=cost(12 * count * width * cols, 6 * width * cols),
        name="last",
    )(a_in, b_in, *rows, *held0, *held1, up_high, down_low)
    last_up0 = lax.ppermute(ul0 + far_up0, "tp", up)
    last_down0 = lax.ppermute(dh0 + far_down0, "tp", down)
    last_up1 = lax.ppermute(ul1 + far_up1, "tp", up)
    last_down1 = lax.ppermute(dh1 + far_down1, "tp", down)
    return pl.pallas_call(
        join_kernel,
        in_specs=[whole()] * 7,
        out_specs=whole(),
        out_shape=jax.ShapeDtypeStruct((count, width), BF16),
        compiler_params=params(12),
        name="join",
    )(own, near_down, near_up, last_up0, last_up1, last_down0, last_down1)


def solution(mesh):
    return jax.shard_map(
        body,
        mesh=mesh,
        in_specs=(
            P("ctx", None),
            P(None, "tp"),
            P(None, "tp"),
            P(None, "tp"),
            P("ctx", "tp"),
            P("ctx"),
        ),
        out_specs=P(("ctx", "tp"), None),
        check_vma=False,
    )
```
